256 devices in a mesh: row: 16 (over y_hi, x, core), col: 16 (over y_lo, z).
Axes of the slice: x: 4, y: 4 (y_hi: 2, y_lo: 2; y = y_hi * 2 + y_lo), z: 8, core: 2. Of those that a mesh axis runs over, the one named last changes fastest.
Arguments:
- amplitudes: bfloat16 [1600, 40960], P('row', 'col'), may hold values from -6 to 6
- integrals: bfloat16 [32768, 40960], P('row', 'col'), may hold values from -0.0390625 to 0.0390625
- row_offsets: int32 [17], replicated, may hold values from 0 to 20438, as said below
- panel_owner: int32 [3], replicated, may hold values from 0 to 15
Outputs:
- residual: float32 [3, 100, 32768], P(None, None, ('row', 'col'))
The draws below stay inside these ranges and needn't reach their ends.
Inputs may be any that keep to these rules, and one draw needn't show every extreme that they name: row_offsets[0] is 0 and they rise; row block q holds row_offsets[q + 1] - row_offsets[q] live rows, from 512 to 2048, in its first slots; block 0 holds exactly 2048.
All inputs are finite; a program needn't handle non-finite values.
Results may differ from the reference program's by a relative error of at most 0.0003.
Values may be sent and summed in bfloat16 or wider, within the bound.
No kernel may reach another device: no remote copies, remote signals or barrier semaphores. Data moves between devices by JAX's collectives and lax.ppermute only.
A program may use at most 64 MiB of HBM per device.

```python
import jax
import jax.numpy as jnp
from jax import lax

CD_DEV = 2560
ROWS_CAP = 2048
STEPS = 3
OO = 1600
PW = 100
CD = 40960
NAB = 32768
N_ROW = 16
N_COL = 16


def draw_row_offsets(key, part):
    lowest = ROWS_CAP // 4
    step_size = (ROWS_CAP - lowest) // (N_ROW - 1)
    spread = step_size
    rank_ids = jnp.arange(N_ROW, dtype=jnp.int32)
    falling = step_size * (N_ROW - 1 - rank_ids)
    jitter = jax.random.randint(key, (N_ROW,), 0, spread + 1).astype(jnp.int32)
    jitter = jnp.where((rank_ids == 0) | (rank_ids == N_ROW - 1), 0, jitter).astype(jnp.int32)
    earlier = jnp.concatenate([jnp.zeros((1,), jnp.int32), jitter[:-1]])
    counts = lowest + falling - jitter + earlier
    counts = jnp.where(rank_ids == 0, ROWS_CAP, counts).astype(jnp.int32)
    return jnp.concatenate([jnp.zeros((1,), jnp.int32), jnp.cumsum(counts).astype(jnp.int32)])


def spiked(drawn, stream_key, source, target, blocks, factor):
    owner, partner = [(jnp.arange(drawn.shape[dim]) // (drawn.shape[dim] // blocks)).reshape([-1 if axis == dim else 1 for axis in range(drawn.ndim)]) for dim in (source, target)]
    chosen = jax.random.permutation(stream_key, blocks)[partner]
    strong = (owner == chosen) | (owner == (partner + blocks // 2) % blocks)
    return jnp.where(strong, factor * drawn, drawn)


def block_scale(own_key, extent, cuts, least, high):
    def one(position, shards_of):
        draws = jax.random.uniform(jax.random.fold_in(jax.random.fold_in(own_key, 6), position), (shards_of,), jnp.float32, least / len(cuts), high / len(cuts))
        return jnp.repeat(jnp.exp(draws), extent[position] // shards_of).reshape((-1,) + (1,) * (len(extent) - position - 1))

    loudness = one(*cuts[0])
    for cut in cuts[1:]:
        loudness = loudness * one(*cut)
    return loudness


def bell_draw(rng, dims, scale, bound, shards=(), kind=jnp.bfloat16):
    result = jax.random.normal(rng, dims, jnp.float32) * scale
    if len(shards) > 0:
        result = block_scale(rng, dims, shards, -0.22, 0.18) * result
    return jnp.clip(result, min=-bound, max=bound).astype(kind)


def heavy_noise(stream_key, dims, scale, reach, split, heavy, kind=jnp.bfloat16):
    drawn = scale * jax.random.normal(stream_key, dims, jnp.float32)
    if split:
        drawn = drawn * block_scale(stream_key, dims, split, -0.22, 0.18)
    return jnp.clip(spiked(drawn, jax.random.fold_in(stream_key, 3), *heavy), -reach, reach).astype(kind)


def setup_inputs(seed: int = 0) -> dict:
    splits = jax.random.split(jax.random.key(seed), 5)
    amplitudes = bell_draw(splits[0], (OO, CD), 1.0, 6.0, ((0, 16), (1, 16)))
    integrals = heavy_noise(splits[1], (NAB, CD), CD ** -0.5, 0.0390625, ((0, 16), (1, 16)), (1, 0, 16, 2.0))
    row_offsets = draw_row_offsets(jax.random.fold_in(splits[4], 71), 0)
    panel_owner = jax.random.randint(splits[3], (STEPS,), 0, N_ROW).astype(jnp.int32)
    return dict(amplitudes=amplitudes, integrals=integrals, row_offsets=row_offsets, panel_owner=panel_owner)


def reference(amplitudes, integrals, row_offsets, panel_owner):
    counts = row_offsets[1:] - row_offsets[:-1]
    slot_ids = jnp.arange(NAB, dtype=jnp.int32)
    owners = slot_ids // ROWS_CAP
    live_mask = ((slot_ids % ROWS_CAP) < counts[owners]).astype(jnp.float32)
    collected = []
    for step in range(STEPS):
        start = (panel_owner[step] * PW).astype(jnp.int32)
        amp_panel = lax.dynamic_slice_in_dim(amplitudes, start, PW, 0)

        def add_block(column_block, summed):
            first = (column_block * CD_DEV).astype(jnp.int32)
            left = lax.dynamic_slice_in_dim(amp_panel, first, CD_DEV, 1)
            right = lax.dynamic_slice_in_dim(integrals, first, CD_DEV, 1)
            part = lax.dot_general(left, right, (((1,), (1,)), ((), ())), preferred_element_type=jnp.float32)
            return summed + part

        summed = lax.fori_loop(0, N_COL, add_block, jnp.zeros((PW, NAB), jnp.float32))
        collected.append(summed * live_mask[None, :])
    return jnp.stack(collected)
```

```python
import jax
import jax.numpy as jnp
from jax import lax
from jax.sharding import Mesh, PartitionSpec as P

STEPS = 3
PW = 100
ROW = ("yh", "x", "core")
COL = ("yl", "z")
SLOT = 128
PADDED = 104
CODE = 14


def shift(size, by):
    return [(i, (i + by) % size) for i in range(size)]


def gather_panels(amplitudes, panel_owner):
    padded = jnp.pad(amplitudes, ((0, 28), (0, 0)))
    pieces = padded.reshape(4, 32, 4, 640).transpose(0, 2, 1, 3).reshape(16, 32, 640)
    held = lax.all_to_all(pieces, ROW, 0, 0)
    mine = jnp.stack([lax.dynamic_index_in_dim(held, panel_owner[s], 0, keepdims=False) for s in range(STEPS)])
    held = jnp.stack([mine, lax.ppermute(mine, "yh", shift(2, 1))])
    held = jnp.stack([held] + [lax.ppermute(held, "x", shift(4, d)) for d in range(1, 4)])
    held = jnp.stack([held, lax.ppermute(held, "core", shift(2, 1))])
    yh, x, core = (lax.axis_index(a) for a in ROW)
    held = lax.dynamic_slice_in_dim(jnp.concatenate([held, held]), core, 2, 0)
    held = held.transpose(1, 2, 0, 3, 4, 5)
    held = held[::-1]
    held = lax.dynamic_slice_in_dim(jnp.concatenate([held, held]), 3 - x, 4, 0)
    held = held.transpose(1, 0, 2, 3, 4, 5)
    held = lax.dynamic_slice_in_dim(jnp.concatenate([held, held]), yh, 2, 0)
    held = held.reshape(4, 4, STEPS, 32, 640).transpose(2, 0, 3, 1, 4).reshape(STEPS, 128, 2560)
    return held[:, :PW]


def per_device(amplitudes, integrals, row_offsets, panel_owner):
    panels = gather_panels(amplitudes, panel_owner)
    product = lax.dot_general(
        panels, integrals, (((2,), (1,)), ((), ())), preferred_element_type=jnp.float32
    )
    term = product.reshape(STEPS, PW, 16, SLOT).transpose(2, 0, 1, 3)
    largest = jnp.max(jnp.abs(term), axis=2, keepdims=True)
    exponent = jnp.floor(jnp.log2(jnp.maximum(largest, 2.0**-100)))
    code = jnp.clip(jnp.round(term * jnp.exp2(CODE - exponent)), -32767, 32767)
    code = jnp.concatenate([code, exponent, jnp.zeros((16, STEPS, PADDED - PW - 1, SLOT), jnp.float32)], axis=2)
    got = lax.all_to_all(code.astype(jnp.int32).astype(jnp.int16), COL, 0, 0)
    got = got.astype(jnp.int32).astype(jnp.float32)
    total = jnp.sum(got[:, :, :PW] * jnp.exp2(got[:, :, PW : PW + 1] - CODE), axis=0)
    own_row = lax.axis_index(ROW)
    live_rows = row_offsets[own_row + 1] - row_offsets[own_row]
    slot = lax.axis_index(COL) * SLOT + jnp.arange(SLOT, dtype=jnp.int32)
    return total * (slot < live_rows).astype(jnp.float32)[None, None, :]


def solution(mesh):
    fine = Mesh(mesh.devices.reshape(2, 4, 2, 2, 8), ROW + COL)
    return jax.shard_map(
        per_device,
        mesh=fine,
        in_specs=(P(ROW, COL), P(ROW, COL), P(), P()),
        out_specs=P(None, None, ROW + COL),
        check_vma=False,
    )
```

```python
import jax
import jax.numpy as jnp
from jax import lax
from jax.experimental import pallas as pl
from jax.experimental.pallas import tpu as pltpu
from jax.sharding import Mesh, PartitionSpec as P

STEPS = 3
ROW = ("yh", "x", "core")
COL = ("yl", "z")
SLOT = 128
RB = 25
BLK = 80
USED = STEPS * RB
KB = 640
CODE = 14
WIDE = 256
VMEM = pl.BlockSpec(memory_space=pltpu.VMEM)
SMEM = pl.BlockSpec(memory_space=pltpu.SMEM)


def shift(size, by):
    return [(i, (i + by) % size) for i in range(size)]


def gather_panels(amplitudes, panel_owner):
    pieces = jnp.pad(amplitudes.reshape(2, 2, RB, 4, KB), ((0, 0), (0, 0), (0, 7), (0, 0), (0, 0)))
    pieces = pieces.transpose(0, 3, 1, 2, 4).reshape(16, 32, KB)
    held = lax.all_to_all(pieces, ROW, 0, 0)
    mine = [lax.dynamic_index_in_dim(held, panel_owner[s], 0, keepdims=False)[:RB] for s in range(STEPS)]
    mine = jnp.concatenate(mine + [jnp.zeros((BLK - USED, KB), mine[0].dtype)])
    two = jnp.stack([mine, lax.ppermute(mine, "yh", shift(2, 1))])
    eight = jnp.stack([two] + [lax.ppermute(two, "x", shift(4, d)) for d in range(1, 4)])
    return eight, lax.ppermute(eight, "core", shift(2, 1))


def encode(block):
    largest = jnp.max(jnp.abs(block), axis=0, keepdims=True)
    exponent = jnp.floor(jnp.log2(jnp.maximum(largest, 2.0**-100)))
    code = jnp.clip(jnp.round(block * jnp.exp2(CODE - exponent)), -32767.0, 32767.0)
    row = lax.broadcasted_iota(jnp.int32, block.shape, 0)
    code = jnp.where(row < USED, code, jnp.where(row == USED, exponent, 0.0))
    return code.astype(jnp.int32).astype(jnp.int16)


def decode(code):
    value = code.astype(jnp.int32).astype(jnp.float32)
    return value * jnp.exp2(value[USED : USED + 1] - CODE)


def product_kernel(place, own, other, integrals, out, acc):
    x = place[0]
    half = 4 * BLK // 2
    for back in range(4):
        columns = pl.ds(pl.multiple_of(lax.rem(x - back + 4, 4) * KB, KB), KB)
        right = integrals[:, columns]
        for core, left in enumerate((own, other)):
            part = lax.dot_general(
                left[back].reshape(half, KB), right, (((1,), (1,)), ((), ())), preferred_element_type=jnp.float32
            )
            at = pl.ds(core * half, half)
            acc[at] = part if back == 0 else acc[at] + part
    for d in range(WIDE // SLOT):
        for b in range(4):
            out[d, b] = encode(acc[pl.ds(b * BLK, BLK), pl.ds(d * SLOT, SLOT)])


def sum_kernel(place, got, live, out):
    yh, core = place[1], place[2]
    for rb in range(4):
        b = lax.rem(core + rb, 2) * 2 + lax.rem(yh + rb // 2, 2)
        total = decode(got[0, b])
        for k in range(1, 16):
            total = total + decode(got[k, b])
        total = total * live[...]
        for s in range(STEPS):
            out[s, pl.ds(rb * RB, RB), :] = total[s * RB : (s + 1) * RB]


def per_device(amplitudes, integrals, row_offsets, panel_owner):
    yh, x, core = (lax.axis_index(a) for a in ROW)
    place = jnp.stack([x, yh, core]).astype(jnp.int32)
    own, other = gather_panels(amplitudes, panel_owner)
    whole = (4, 2, BLK, KB)
    codes = pl.pallas_call(
        product_kernel,
        out_shape=jax.ShapeDtypeStruct((16, 4, BLK, SLOT), jnp.int16),
        grid=(16 * SLOT // WIDE,),
        in_specs=[
            SMEM,
            pl.BlockSpec(whole, lambda n: (0, 0, 0, 0)),
            pl.BlockSpec(whole, lambda n: (0, 0, 0, 0)),
            pl.BlockSpec((WIDE, 4 * KB), lambda n: (n, 0)),
        ],
        out_specs=pl.BlockSpec((WIDE // SLOT, 4, BLK, SLOT), lambda n: (n, 0, 0, 0)),
        scratch_shapes=[pltpu.VMEM((4 * BLK, WIDE), jnp.float32)],
        compiler_params=pltpu.CompilerParams(vmem_limit_bytes=56 << 20),
        name="product",
    )(place, own, other, integrals)
    got = lax.all_to_all(codes, COL, 0, 0)
    own_row = lax.axis_index(ROW)
    slot = lax.axis_index(COL) * SLOT + jnp.arange(SLOT, dtype=jnp.int32)
    live = (slot < row_offsets[own_row + 1] - row_offsets[own_row]).astype(jnp.float32)[None, :]
    return pl.pallas_call(
        sum_kernel,
        out_shape=jax.ShapeDtypeStruct((STEPS, 4 * RB, SLOT), jnp.float32),
        in_specs=[SMEM, VMEM, VMEM],
        out_specs=VMEM,
        compiler_params=pltpu.CompilerParams(vmem_limit_bytes=8 << 20),
        name="sum",
    )(place, got, live)


def solution(mesh):
    fine = Mesh(mesh.devices.reshape(2, 4, 2, 2, 8), ROW + COL)
    return jax.shard_map(
        per_device,
        mesh=fine,
        in_specs=(P(ROW, COL), P(ROW, COL), P(), P()),
        out_specs=P(None, None, ROW + COL),
        check_vma=False,
    )
```

```python
import jax
import jax.numpy as jnp
from jax import lax
from jax.experimental import pallas as pl
from jax.experimental.pallas import tpu as pltpu
from jax.sharding import Mesh, PartitionSpec as P

STEPS = 3
ROW = ("yh", "x", "core")
COL = ("yl", "z")
SLOT = 128
RB = 25
USED = STEPS * RB
BLK = 80
ROWS = 4 * USED
TALL = 304
GROUPS = ((0, 80), (80, 160), (160, 240), (240, TALL))
KB = 640
WIDE = 512
SLABS = 4
CODE = 2.0**14 * (1 - 2.0**-13)
VMEM = pl.BlockSpec(memory_space=pltpu.VMEM)
SMEM = pl.BlockSpec(memory_space=pltpu.SMEM)
HBM = pl.BlockSpec(memory_space=pltpu.HBM)
SMALL = pltpu.CompilerParams(vmem_limit_bytes=8 << 20)
LARGE = pltpu.CompilerParams(vmem_limit_bytes=54 << 20)


def shift(size, by):
    return [(i, (i + by) % size) for i in range(size)]


def cut_kernel(panel, pieces):
    for yh in range(2):
        for core in range(2):
            rows = slice((yh * 2 + core) * RB, (yh * 2 + core + 1) * RB)
            for x in range(4):
                pieces[yh * 8 + x * 2 + core, pl.ds(0, RB), :] = panel[rows, x * KB : (x + 1) * KB]


def pick_kernel(owner, held, mine):
    for s in range(STEPS):
        mine[pl.ds(s * RB, RB), :] = held[owner[s], pl.ds(0, RB), :]


def gather_panels(amplitudes, panel_owner):
    pieces = pl.pallas_call(
        cut_kernel,
        out_shape=jax.ShapeDtypeStruct((16, 32, KB), jnp.bfloat16),
        in_specs=[VMEM],
        out_specs=VMEM,
        compiler_params=SMALL,
        name="cut",
    )(amplitudes)
    held = lax.all_to_all(pieces, ROW, 0, 0)
    mine = pl.pallas_call(
        pick_kernel,
        out_shape=jax.ShapeDtypeStruct((BLK, KB), jnp.bfloat16),
        in_specs=[SMEM, VMEM],
        out_specs=VMEM,
        compiler_params=SMALL,
        name="pick",
    )(panel_owner, held)
    two = jnp.stack([mine, lax.ppermute(mine, "yh", shift(2, 1))])
    eight = jnp.stack([two] + [lax.ppermute(two, "x", shift(4, d)) for d in range(1, 4)])
    return eight, lax.ppermute(eight, "core", shift(2, 1))


def encode(rows, out, at):
    exponents = []
    for lo, hi in GROUPS:
        block = rows(lo, hi)
        largest = jnp.max(jnp.abs(block), axis=0, keepdims=True)
        exponent = jnp.floor(jnp.log2(jnp.maximum(largest, 2.0**-100)))
        exponents.append(exponent)
        code = jnp.round(block * (jnp.exp2(-exponent) * CODE))
        if hi == TALL:
            row = lax.broadcasted_iota(jnp.int32, (16, SLOT), 0) + TALL - 16
            last = code[-16:]
            for g, e in enumerate(exponents):
                last = jnp.where(row == ROWS + g, e, last)
            code = jnp.concatenate([code[:-16], last])
        out[at, pl.ds(lo, hi - lo), :] = code.astype(jnp.int32).astype(jnp.int16)


def decode(codes, lo, hi, group):
    scale = jnp.exp2(codes[pl.ds(TALL - 16, 16), :].astype(jnp.int32).astype(jnp.float32)[12 + group : 13 + group])
    return codes[pl.ds(lo, hi - lo), :].astype(jnp.int32).astype(jnp.float32) * (scale * (1 / CODE))


def product_kernel(own, other, integrals, out, left, slabs, acc, sems):
    x = lax.axis_index("x")
    copies = []
    for n in range(SLABS):
        copies.append(pltpu.make_async_copy(integrals.at[pl.ds(n * WIDE, WIDE)], slabs.at[n], sems.at[n]))
        copies[-1].start()
    left[pl.ds(TALL - 16, 16), :] = jnp.zeros((16, 4 * KB), jnp.bfloat16)
    for back in range(4):
        columns = pl.ds(pl.multiple_of(lax.rem(x - back + 4, 4) * KB, KB), KB)
        for core, piece in enumerate((own, other)):
            for yh in range(2):
                left[pl.ds((core * 2 + yh) * USED, USED), columns] = piece[back, yh, pl.ds(0, USED), :]
    for n in range(SLABS):
        copies[n].wait()
        acc[n % 2] = lax.dot_general(
            left[...], slabs[n], (((1,), (1,)), ((), ())), preferred_element_type=jnp.float32
        )
        for d in range(WIDE // SLOT):
            encode(lambda lo, hi: acc[n % 2, pl.ds(lo, hi - lo), pl.ds(d * SLOT, SLOT)], out, n * 4 + d)


def sum_kernel(got, live, out, total):
    yh, core = lax.axis_index("yh"), lax.axis_index("core")
    for g, (lo, hi) in enumerate(GROUPS):
        part = decode(got.at[0], lo, hi, g)
        for k in range(1, 16):
            part = part + decode(got.at[k], lo, hi, g)
        total[pl.ds(lo, hi - lo), :] = part * live[...]
    for b in range(4):
        rb = lax.rem(yh + b % 2, 2) * 2 + lax.rem(core + b // 2, 2)
        for case in range(4):

            @pl.when(rb == case)
            def _():
                for s in range(STEPS):
                    out[s, pl.ds(case * RB, RB), :] = total[pl.ds(b * USED + s * RB, RB), :]


def per_device(amplitudes, integrals, row_offsets, panel_owner):
    own, other = gather_panels(amplitudes, panel_owner)
    codes = pl.pallas_call(
        product_kernel,
        out_shape=jax.ShapeDtypeStruct((16, TALL, SLOT), jnp.int16),
        in_specs=[VMEM, VMEM, HBM],
        out_specs=VMEM,
        scratch_shapes=[
            pltpu.VMEM((TALL, 4 * KB), jnp.bfloat16),
            pltpu.VMEM((SLABS, WIDE, 4 * KB), jnp.bfloat16),
            pltpu.VMEM((2, TALL, WIDE), jnp.float32),
            pltpu.SemaphoreType.DMA((SLABS,)),
        ],
        compiler_params=LARGE,
        name="product",
    )(own, other, integrals)
    got = lax.all_to_all(codes, COL, 0, 0)
    own_row = lax.axis_index(ROW)
    slot = lax.axis_index(COL) * SLOT + jnp.arange(SLOT, dtype=jnp.int32)
    live = (slot < row_offsets[own_row + 1] - row_offsets[own_row]).astype(jnp.float32)[None, :]
    return pl.pallas_call(
        sum_kernel,
        out_shape=jax.ShapeDtypeStruct((STEPS, 4 * RB, SLOT), jnp.float32),
        in_specs=[VMEM, VMEM],
        out_specs=VMEM,
        scratch_shapes=[pltpu.VMEM((TALL, SLOT), jnp.float32)],
        compiler_params=SMALL,
        name="sum",
    )(got, live)


def solution(mesh):
    fine = Mesh(mesh.devices.reshape(2, 4, 2, 2, 8), ROW + COL)
    return jax.shard_map(
        per_device,
        mesh=fine,
        in_specs=(P(ROW, COL), P(ROW, COL), P(), P()),
        out_specs=P(None, None, ROW + COL),
        check_vma=False,
    )
```

```python
import jax
import jax.numpy as jnp
from jax import lax
from jax.experimental import pallas as pl
from jax.experimental.pallas import tpu as pltpu
from jax.sharding import Mesh, PartitionSpec as P

STEPS = 3
ROW = ("yh", "x", "core")
COL = ("yl", "z")
SLOT = 128
RB = 25
USED = STEPS * RB
BLK = 80
ROWS = 4 * USED
TALL = 304
GROUPS = ((0, 80), (80, 160), (160, 240), (240, TALL))
KB = 640
TILES = KB // 128
WIDE = 512
SLABS = 4
CODE = 2.0**14 * (1 - 2.0**-13)
VMEM = pl.BlockSpec(memory_space=pltpu.VMEM)
SMEM = pl.BlockSpec(memory_space=pltpu.SMEM)
HBM = pl.BlockSpec(memory_space=pltpu.HBM)
SMALL = pltpu.CompilerParams(vmem_limit_bytes=8 << 20)
LARGE = pltpu.CompilerParams(vmem_limit_bytes=46 << 20)


def shift(size, by):
    return [(i, (i + by) % size) for i in range(size)]


def cut_kernel(panel, pieces):
    for yh in range(2):
        for core in range(2):
            for x in range(4):
                for t in range(TILES):
                    block = panel[pl.ds((yh * 2 + core) * RB, RB), pl.ds(x * KB + t * 128, 128)]
                    pieces[yh * 8 + x * 2 + core, pl.ds(t * RB, RB), :] = block


def pick_kernel(owner, held, mine):
    for s in range(STEPS):
        for t in range(TILES):
            mine[pl.ds(s * RB, RB), pl.ds(t * 128, 128)] = held[owner[s], pl.ds(t * RB, RB), :]


def gather_panels(amplitudes, panel_owner):
    pieces = pl.pallas_call(
        cut_kernel,
        out_shape=jax.ShapeDtypeStruct((16, 128, 128), jnp.bfloat16),
        in_specs=[VMEM],
        out_specs=VMEM,
        compiler_params=SMALL,
        name="cut",
    )(amplitudes)
    held = lax.all_to_all(pieces, ROW, 0, 0)
    mine = pl.pallas_call(
        pick_kernel,
        out_shape=jax.ShapeDtypeStruct((BLK, KB), jnp.bfloat16),
        in_specs=[SMEM, VMEM],
        out_specs=VMEM,
        compiler_params=SMALL,
        name="pick",
    )(panel_owner, held)
    two = jnp.stack([mine, lax.ppermute(mine, "yh", shift(2, 1))])
    eight = jnp.stack([two] + [lax.ppermute(two, "x", shift(4, d)) for d in range(1, 4)])
    return eight, lax.ppermute(eight, "core", shift(2, 1))


def encode(rows, out, at):
    exponents = []
    for lo, hi in GROUPS:
        block = rows(lo, hi)
        largest = jnp.max(jnp.abs(block), axis=0, keepdims=True)
        exponent = jnp.floor(jnp.log2(jnp.maximum(largest, 2.0**-100)))
        exponents.append(exponent)
        code = jnp.round(block * (jnp.exp2(-exponent) * CODE))
        if hi == TALL:
            row = lax.broadcasted_iota(jnp.int32, (16, SLOT), 0) + TALL - 16
            last = code[-16:]
            for g, e in enumerate(exponents):
                last = jnp.where(row == ROWS + g, e, last)
            code = jnp.concatenate([code[:-16], last])
        out[at, pl.ds(lo, hi - lo), :] = code.astype(jnp.int32).astype(jnp.int16)


def decode(codes, lo, hi, group):
    scale = jnp.exp2(codes[pl.ds(TALL - 16, 16), :].astype(jnp.int32).astype(jnp.float32)[12 + group : 13 + group])
    return codes[pl.ds(lo, hi - lo), :].astype(jnp.int32).astype(jnp.float32) * (scale * (1 / CODE))


def product_kernel(own, other, integrals, out, left, slabs, acc, sems):
    x = lax.axis_index("x")
    copies = []
    for n in range(SLABS):
        copies.append(pltpu.make_async_copy(integrals.at[pl.ds(n * WIDE, WIDE)], slabs.at[n], sems.at[n]))
        copies[-1].start()
    left[pl.ds(TALL - 16, 16), :] = jnp.zeros((16, 4 * KB), jnp.bfloat16)
    for back in range(4):
        columns = pl.ds(pl.multiple_of(lax.rem(x - back + 4, 4) * KB, KB), KB)
        for core, piece in enumerate((own, other)):
            for yh in range(2):
                left[pl.ds((core * 2 + yh) * USED, USED), columns] = piece[back, yh, pl.ds(0, USED), :]
    for n in range(SLABS):
        copies[n].wait()
        acc[n % 2] = lax.dot_general(
            left[...], slabs[n], (((1,), (1,)), ((), ())), preferred_element_type=jnp.float32
        )
        for d in range(WIDE // SLOT):
            encode(lambda lo, hi: acc[n % 2, pl.ds(lo, hi - lo), pl.ds(d * SLOT, SLOT)], out, n * 4 + d)


def sum_kernel(got, live, out, total):
    yh, core = lax.axis_index("yh"), lax.axis_index("core")
    for g, (lo, hi) in enumerate(GROUPS):
        part = decode(got.at[0], lo, hi, g)
        for k in range(1, 16):
            part = part + decode(got.at[k], lo, hi, g)
        total[pl.ds(lo, hi - lo), :] = part * live[...]
    for b in range(4):
        rb = lax.rem(yh + b % 2, 2) * 2 + lax.rem(core + b // 2, 2)
        for case in range(4):

            @pl.when(rb == case)
            def _():
                for s in range(STEPS):
                    out[s, pl.ds(case * RB, RB), :] = total[pl.ds(b * USED + s * RB, RB), :]


def per_device(amplitudes, integrals, row_offsets, panel_owner):
    own, other = gather_panels(amplitudes, panel_owner)
    codes = pl.pallas_call(
        product_kernel,
        out_shape=jax.ShapeDtypeStruct((16, TALL, SLOT), jnp.int16),
        in_specs=[VMEM, VMEM, HBM],
        out_specs=VMEM,
        scratch_shapes=[
            pltpu.VMEM((TALL, 4 * KB), jnp.bfloat16),
            pltpu.VMEM((SLABS, WIDE, 4 * KB), jnp.bfloat16),
            pltpu.VMEM((2, TALL, WIDE), jnp.float32),
            pltpu.SemaphoreType.DMA((SLABS,)),
        ],
        compiler_params=LARGE,
        name="product",
    )(own, other, integrals)
    got = lax.all_to_all(codes, COL, 0, 0)
    own_row = lax.axis_index(ROW)
    slot = lax.axis_index(COL) * SLOT + jnp.arange(SLOT, dtype=jnp.int32)
    live = (slot < row_offsets[own_row + 1] - row_offsets[own_row]).astype(jnp.float32)[None, :]
    return pl.pallas_call(
        sum_kernel,
        out_shape=jax.ShapeDtypeStruct((STEPS, 4 * RB, SLOT), jnp.float32),
        in_specs=[VMEM, VMEM],
        out_specs=VMEM,
        scratch_shapes=[pltpu.VMEM((TALL, SLOT), jnp.float32)],
        compiler_params=SMALL,
        name="sum",
    )(got, live)


def solution(mesh):
    fine = Mesh(mesh.devices.reshape(2, 4, 2, 2, 8), ROW + COL)
    return jax.shard_map(
        per_device,
        mesh=fine,
        in_specs=(P(ROW, COL), P(ROW, COL), P(), P()),
        out_specs=P(None, None, ROW + COL),
        check_vma=False,
    )
```

```python
import jax
import jax.numpy as jnp
from jax import lax
from jax.experimental import pallas as pl
from jax.experimental.pallas import tpu as pltpu
from jax.sharding import Mesh, PartitionSpec as P

STEPS = 3
ROW = ("yh", "x", "core")
COL = ("yl", "z")
SLOT = 128
RB = 25
USED = STEPS * RB
BLK = 80
ROWS = 4 * USED
TALL = 304
GROUPS = ((0, 80), (80, 160), (160, 240), (240, TALL))
KB = 640
TILES = KB // 128
FAR = (4, 3, 5)
NEAR = (2, 6, 1, 7, 0)
CODE = 2.0**14 * (1 - 2.0**-13)
VMEM = pl.BlockSpec(memory_space=pltpu.VMEM)
SMEM = pl.BlockSpec(memory_space=pltpu.SMEM)
HBM = pl.BlockSpec(memory_space=pltpu.HBM)
ANY = pl.BlockSpec(memory_space=pl.ANY)
SMALL = pltpu.CompilerParams(vmem_limit_bytes=8 << 20)
LARGE = pltpu.CompilerParams(vmem_limit_bytes=46 << 20)


def shift(size, by):
    return [(i, (i + by) % size) for i in range(size)]


def cut_kernel(panel, pieces):
    for yh in range(2):
        for core in range(2):
            for x in range(4):
                for t in range(TILES):
                    block = panel[pl.ds((yh * 2 + core) * RB, RB), pl.ds(x * KB + t * 128, 128)]
                    pieces[yh * 8 + x * 2 + core, pl.ds(t * RB, RB), :] = block


def pick_kernel(owner, held, mine):
    for s in range(STEPS):
        for t in range(TILES):
            mine[pl.ds(s * RB, RB), pl.ds(t * 128, 128)] = held[owner[s], pl.ds(t * RB, RB), :]


def gather_panels(amplitudes, panel_owner):
    pieces = pl.pallas_call(
        cut_kernel,
        out_shape=jax.ShapeDtypeStruct((16, 128, 128), jnp.bfloat16),
        in_specs=[VMEM],
        out_specs=VMEM,
        compiler_params=SMALL,
        name="cut",
    )(amplitudes)
    held = lax.all_to_all(pieces, ROW, 0, 0)
    mine = pl.pallas_call(
        pick_kernel,
        out_shape=jax.ShapeDtypeStruct((BLK, KB), jnp.bfloat16),
        in_specs=[SMEM, VMEM],
        out_specs=VMEM,
        compiler_params=SMALL,
        name="pick",
    )(panel_owner, held)
    two = jnp.stack([mine, lax.ppermute(mine, "yh", shift(2, 1))])
    eight = jnp.stack([two] + [lax.ppermute(two, "x", shift(4, d)) for d in range(1, 4)])
    return eight, lax.ppermute(eight, "core", shift(2, 1))


def last_rows():
    return lax.broadcasted_iota(jnp.int32, (16, SLOT), 0) + TALL - 16


def encode(rows, out, at):
    exponents = []
    for lo, hi in GROUPS:
        block = rows(lo, hi)
        largest = jnp.max(jnp.abs(block), axis=0, keepdims=True)
        exponent = jnp.floor(jnp.log2(jnp.maximum(largest, 2.0**-100)))
        exponents.append(exponent)
        code = jnp.round(block * (jnp.exp2(-exponent) * CODE))
        if hi == TALL:
            last = code[-16:]
            for g, e in enumerate(exponents):
                last = jnp.where(last_rows() == ROWS + g, e, last)
            code = jnp.concatenate([code[:-16], last])
        rows_out = (pl.ds(lo, hi - lo), slice(None))
        out[rows_out if at is None else (at,) + rows_out] = code.astype(jnp.int32).astype(jnp.int16)


def decode(codes, lo, hi, group):
    scale = jnp.exp2(codes[pl.ds(TALL - 16, 16), :].astype(jnp.int32).astype(jnp.float32)[12 + group : 13 + group])
    return codes[pl.ds(lo, hi - lo), :].astype(jnp.int32).astype(jnp.float32) * (scale * (1 / CODE))


def fetch(integrals, slabs, sems, yl, places):
    z = lax.axis_index("z")
    copies = []
    for n, d in enumerate(places):
        rows = pl.ds(pl.multiple_of((yl * 8 + lax.rem(z + d, 8)) * SLOT, SLOT), SLOT)
        copies.append(pltpu.make_async_copy(integrals.at[rows], slabs.at[pl.ds(n * SLOT, SLOT)], sems.at[n]))
        copies[-1].start()
    return copies


def multiply(left, slabs, copies, acc):
    count, n = len(copies), 0
    for some in (count - 3 * ((count - 1) // 3),) + (3,) * ((count - 1) // 3):
        for copy in copies[n : n + some]:
            copy.wait()
        columns = pl.ds(n * SLOT, some * SLOT)
        acc[:, columns] = lax.dot_general(
            left[...], slabs[columns, :], (((1,), (1,)), ((), ())), preferred_element_type=jnp.float32
        )
        n += some


def encode_all(acc, out):
    for n in range(out.shape[0]):
        encode(lambda lo, hi: acc[pl.ds(lo, hi - lo), pl.ds(n * SLOT, SLOT)], out, n)


def away_far_kernel(own, other, integrals, out, left, slabs, acc, sems):
    x = lax.axis_index("x")
    copies = fetch(integrals, slabs, sems, 1 - lax.axis_index("yl"), FAR)
    left[pl.ds(TALL - 16, 16), :] = jnp.zeros((16, 4 * KB), jnp.bfloat16)
    for back in range(4):
        columns = pl.ds(pl.multiple_of(lax.rem(x - back + 4, 4) * KB, KB), KB)
        for core, piece in enumerate((own, other)):
            for yh in range(2):
                left[pl.ds((core * 2 + yh) * USED, USED), columns] = piece[back, yh, pl.ds(0, USED), :]
    multiply(left, slabs, copies, acc)
    encode_all(acc, out)


def away_near_kernel(left, integrals, out, slabs, acc, sems):
    multiply(left, slabs, fetch(integrals, slabs, sems, 1 - lax.axis_index("yl"), NEAR), acc)
    encode_all(acc, out)


def home_kernel(left, integrals, after, out, slabs, sems):
    multiply(left, slabs, fetch(integrals, slabs, sems, lax.axis_index("yl"), FAR + NEAR), out)


def added(got, kept, n, column):
    sums = []
    for g, (lo, hi) in enumerate(GROUPS):
        part = kept[pl.ds(lo, hi - lo), pl.ds(column * SLOT, SLOT)] + decode(got.at[n], lo, hi, g)
        if hi == TALL:
            part = jnp.concatenate([part[:-16], jnp.where(last_rows() < ROWS, part[-16:], 0.0)])
        sums.append(part)
    return sums


def meet_far_kernel(got, kept, *outs):
    for n, out in enumerate(outs):
        sums = added(got, kept, n, n)
        encode(lambda lo, hi: sums[GROUPS.index((lo, hi))], out, None)


def meet_near_kernel(got, kept, after, *outs):
    for n, out in enumerate(outs):
        sums = added(got, kept, n, len(FAR) + n)
        if NEAR[n] == 0:
            for (lo, hi), part in zip(GROUPS, sums):
                out[pl.ds(lo, hi - lo), :] = part
        else:
            encode(lambda lo, hi: sums[GROUPS.index((lo, hi))], out, None)


def sum_kernel(*refs):
    offsets, *got, kept, out, total = refs
    yh, x, core, yl, z = (lax.axis_index(a) for a in ROW + COL)
    row = (yh * 4 + x) * 2 + core
    slot = (yl * 8 + z) * SLOT + lax.broadcasted_iota(jnp.int32, (1, SLOT), 1)
    live = (slot < offsets[row + 1] - offsets[row]).astype(jnp.float32)
    for g, (lo, hi) in enumerate(GROUPS):
        part = kept[pl.ds(lo, hi - lo), :]
        for codes in got:
            part = part + decode(codes, lo, hi, g)
        total[pl.ds(lo, hi - lo), :] = part * live
    for b in range(4):
        rb = lax.rem(yh + b % 2, 2) * 2 + lax.rem(core + b // 2, 2)
        for case in range(4):

            @pl.when(rb == case)
            def _():
                for s in range(STEPS):
                    out[s, pl.ds(case * RB, RB), :] = total[pl.ds(b * USED + s * RB, RB), :]


def per_device(amplitudes, integrals, row_offsets, panel_owner):
    own, other = gather_panels(amplitudes, panel_owner)
    def codes(*n):
        return jax.ShapeDtypeStruct(n + (TALL, SLOT), jnp.int16)

    def cost(n):
        return pl.CostEstimate(
            flops=2 * TALL * 4 * KB * n * SLOT, bytes_accessed=8 * KB * n * SLOT, transcendentals=0
        )

    def room(n):
        return [pltpu.VMEM((n * SLOT, 4 * KB), jnp.bfloat16)]

    def wide(n):
        return [pltpu.VMEM((TALL, n * SLOT), jnp.float32)]

    def sems(n):
        return [pltpu.SemaphoreType.DMA((n,))]

    far, near = len(FAR), len(NEAR)
    away_far, left = pl.pallas_call(
        away_far_kernel,
        out_shape=[codes(far), jax.ShapeDtypeStruct((TALL, 4 * KB), jnp.bfloat16)],
        in_specs=[VMEM, VMEM, HBM],
        out_specs=[VMEM, VMEM],
        scratch_shapes=room(far) + wide(far) + sems(far),
        compiler_params=LARGE,
        cost_estimate=cost(far),
        name="away_far",
    )(own, other, integrals)
    got_far = lax.ppermute(away_far, "yl", shift(2, 1))
    away_near = pl.pallas_call(
        away_near_kernel,
        out_shape=codes(near),
        in_specs=[VMEM, HBM],
        out_specs=VMEM,
        scratch_shapes=room(near) + wide(near) + sems(near),
        compiler_params=LARGE,
        cost_estimate=cost(near),
        name="away_near",
    )(left, integrals)
    kept = pl.pallas_call(
        home_kernel,
        out_shape=jax.ShapeDtypeStruct((TALL, 8 * SLOT), jnp.float32),
        in_specs=[VMEM, HBM, ANY],
        out_specs=VMEM,
        scratch_shapes=room(8) + sems(8),
        compiler_params=LARGE,
        cost_estimate=cost(8),
        name="home",
    )(left, integrals, away_near)
    got_far, away_near, kept = lax.optimization_barrier((got_far, away_near, kept))
    got_near = lax.ppermute(away_near, "yl", shift(2, 1))
    met_far = pl.pallas_call(
        meet_far_kernel,
        out_shape=[codes()] * far,
        in_specs=[VMEM, VMEM],
        out_specs=[VMEM] * far,
        compiler_params=SMALL,
        name="meet_far",
    )(got_far, kept)
    met_near = pl.pallas_call(
        meet_near_kernel,
        out_shape=[codes()] * (near - 1) + [jax.ShapeDtypeStruct((TALL, SLOT), jnp.float32)],
        in_specs=[VMEM, VMEM, ANY],
        out_specs=[VMEM] * near,
        compiler_params=SMALL,
        name="meet_near",
    )(got_near, kept, met_far[0])
    got = [lax.ppermute(c, "z", shift(8, d)) for c, d in zip(met_far, FAR)]
    got += [lax.ppermute(c, "z", shift(8, d)) for c, d in zip(met_near, NEAR[:-1])]
    return pl.pallas_call(
        sum_kernel,
        out_shape=jax.ShapeDtypeStruct((STEPS, 4 * RB, SLOT), jnp.float32),
        in_specs=[SMEM] + [VMEM] * 8,
        out_specs=VMEM,
        scratch_shapes=[pltpu.VMEM((TALL, SLOT), jnp.float32)],
        compiler_params=SMALL,
        name="sum",
    )(row_offsets, *got, met_near[-1])


def solution(mesh):
    fine = Mesh(mesh.devices.reshape(2, 4, 2, 2, 8), ROW + COL)
    return jax.shard_map(
        per_device,
        mesh=fine,
        in_specs=(P(ROW, COL), P(ROW, COL), P(), P()),
        out_specs=P(None, None, ROW + COL),
        check_vma=False,
    )
```

```python
import jax
import jax.numpy as jnp
from jax import lax
from jax.experimental import pallas as pl
from jax.experimental.pallas import tpu as pltpu
from jax.sharding import Mesh, PartitionSpec as P

STEPS = 3
ROW = ("yh", "x", "core")
COL = ("yl", "z")
SLOT = 128
RB = 25
USED = STEPS * RB
BLK = 80
ROWS = 4 * USED
TALL = 304
GROUPS = ((0, 80), (80, 160), (160, 240), (240, TALL))
KB = 640
TILES = KB // 128
FAR = (4, 3, 5)
NEAR = (2, 6, 1, 7, 0)
CODE = 2.0**14 * (1 - 2.0**-13)
VMEM = pl.BlockSpec(memory_space=pltpu.VMEM)
SMEM = pl.BlockSpec(memory_space=pltpu.SMEM)
HBM = pl.BlockSpec(memory_space=pltpu.HBM)
ANY = pl.BlockSpec(memory_space=pl.ANY)
SMALL = pltpu.CompilerParams(vmem_limit_bytes=8 << 20)
LARGE = pltpu.CompilerParams(vmem_limit_bytes=46 << 20)


def shift(size, by):
    return [(i, (i + by) % size) for i in range(size)]


def cut_kernel(panel, pieces):
    for yh in range(2):
        for core in range(2):
            for x in range(4):
                for t in range(TILES):
                    block = panel[pl.ds((yh * 2 + core) * RB, RB), pl.ds(x * KB + t * 128, 128)]
                    pieces[yh * 8 + x * 2 + core, pl.ds(t * RB, RB), :] = block


def pick_kernel(owner, held, mine):
    for s in range(STEPS):
        for t in range(TILES):
            mine[pl.ds(s * RB, RB), pl.ds(t * 128, 128)] = held[owner[s], pl.ds(t * RB, RB), :]


def gather_panels(amplitudes, panel_owner):
    pieces = pl.pallas_call(
        cut_kernel,
        out_shape=jax.ShapeDtypeStruct((16, 128, 128), jnp.bfloat16),
        in_specs=[VMEM],
        out_specs=VMEM,
        compiler_params=SMALL,
        name="cut",
    )(amplitudes)
    held = lax.all_to_all(pieces, ROW, 0, 0)
    mine = pl.pallas_call(
        pick_kernel,
        out_shape=jax.ShapeDtypeStruct((BLK, KB), jnp.bfloat16),
        in_specs=[SMEM, VMEM],
        out_specs=VMEM,
        compiler_params=SMALL,
        name="pick",
    )(panel_owner, held)
    across = lax.ppermute(mine, "yh", shift(2, 1))
    straight = [mine] + [lax.ppermute(mine, "x", shift(4, d)) for d in range(1, 4)]
    turned = [across] + [lax.ppermute(across, "x", shift(4, d)) for d in range(1, 4)]
    eight = jnp.stack([jnp.stack(pair) for pair in zip(straight, turned)])
    return eight, lax.ppermute(eight, "core", shift(2, 1))


def last_rows():
    return lax.broadcasted_iota(jnp.int32, (16, SLOT), 0) + TALL - 16


def encode(rows, out, at):
    exponents = []
    for lo, hi in GROUPS:
        block = rows(lo, hi)
        largest = jnp.max(jnp.abs(block), axis=0, keepdims=True)
        exponent = jnp.floor(jnp.log2(jnp.maximum(largest, 2.0**-100)))
        exponents.append(exponent)
        code = jnp.round(block * (jnp.exp2(-exponent) * CODE))
        if hi == TALL:
            last = code[-16:]
            for g, e in enumerate(exponents):
                last = jnp.where(last_rows() == ROWS + g, e, last)
            code = jnp.concatenate([code[:-16], last])
        rows_out = (pl.ds(lo, hi - lo), slice(None))
        out[rows_out if at is None else (at,) + rows_out] = code.astype(jnp.int32).astype(jnp.int16)


def decode(codes, lo, hi, group):
    scale = jnp.exp2(codes[pl.ds(TALL - 16, 16), :].astype(jnp.int32).astype(jnp.float32)[12 + group : 13 + group])
    return codes[pl.ds(lo, hi - lo), :].astype(jnp.int32).astype(jnp.float32) * (scale * (1 / CODE))


def fetch(integrals, slabs, sems, yl, places):
    z = lax.axis_index("z")
    copies = []
    for n, d in enumerate(places):
        rows = pl.ds(pl.multiple_of((yl * 8 + lax.rem(z + d, 8)) * SLOT, SLOT), SLOT)
        copies.append(pltpu.make_async_copy(integrals.at[rows], slabs.at[pl.ds(n * SLOT, SLOT)], sems.at[n]))
        copies[-1].start()
    return copies


def multiply(left, slabs, copies, acc):
    count, n = len(copies), 0
    for some in (count - 3 * ((count - 1) // 3),) + (3,) * ((count - 1) // 3):
        for copy in copies[n : n + some]:
            copy.wait()
        columns = pl.ds(n * SLOT, some * SLOT)
        acc[:, columns] = lax.dot_general(
            left[...], slabs[columns, :], (((1,), (1,)), ((), ())), preferred_element_type=jnp.float32
        )
        n += some


def encode_all(acc, out):
    for n in range(out.shape[0]):
        encode(lambda lo, hi: acc[pl.ds(lo, hi - lo), pl.ds(n * SLOT, SLOT)], out, n)


def away_far_kernel(own, other, integrals, out, left, slabs, acc, sems):
    x = lax.axis_index("x")
    copies = fetch(integrals, slabs, sems, 1 - lax.axis_index("yl"), FAR)
    left[pl.ds(TALL - 16, 16), :] = jnp.zeros((16, 4 * KB), jnp.bfloat16)
    for back in range(4):
        columns = pl.ds(pl.multiple_of(lax.rem(x - back + 4, 4) * KB, KB), KB)
        for core, piece in enumerate((own, other)):
            for yh in range(2):
                left[pl.ds((core * 2 + yh) * USED, USED), columns] = piece[back, yh, pl.ds(0, USED), :]
    multiply(left, slabs, copies, acc)
    encode_all(acc, out)


def away_near_kernel(left, integrals, out, slabs, acc, sems):
    multiply(left, slabs, fetch(integrals, slabs, sems, 1 - lax.axis_index("yl"), NEAR), acc)
    encode_all(acc, out)


def home_kernel(left, integrals, after, out, slabs, sems):
    multiply(left, slabs, fetch(integrals, slabs, sems, lax.axis_index("yl"), FAR + NEAR), out)


def added(got, kept, n, column):
    sums = []
    for g, (lo, hi) in enumerate(GROUPS):
        part = kept[pl.ds(lo, hi - lo), pl.ds(column * SLOT, SLOT)] + decode(got.at[n], lo, hi, g)
        if hi == TALL:
            part = jnp.concatenate([part[:-16], jnp.where(last_rows() < ROWS, part[-16:], 0.0)])
        sums.append(part)
    return sums


def meet_far_kernel(got, kept, *outs):
    for n, out in enumerate(outs):
        sums = added(got, kept, n, n)
        encode(lambda lo, hi: sums[GROUPS.index((lo, hi))], out, None)


def meet_near_kernel(got, kept, after, *outs):
    for n, out in enumerate(outs):
        sums = added(got, kept, n, len(FAR) + n)
        if NEAR[n] == 0:
            for (lo, hi), part in zip(GROUPS, sums):
                out[pl.ds(lo, hi - lo), :] = part
        else:
            encode(lambda lo, hi: sums[GROUPS.index((lo, hi))], out, None)


def sum_kernel(*refs):
    offsets, *got, kept, out, total = refs
    yh, x, core, yl, z = (lax.axis_index(a) for a in ROW + COL)
    row = (yh * 4 + x) * 2 + core
    slot = (yl * 8 + z) * SLOT + lax.broadcasted_iota(jnp.int32, (1, SLOT), 1)
    live = (slot < offsets[row + 1] - offsets[row]).astype(jnp.float32)
    for g, (lo, hi) in enumerate(GROUPS):
        part = kept[pl.ds(lo, hi - lo), :]
        for codes in got:
            part = part + decode(codes, lo, hi, g)
        total[pl.ds(lo, hi - lo), :] = part * live
    for b in range(4):
        rb = lax.rem(yh + b % 2, 2) * 2 + lax.rem(core + b // 2, 2)
        for case in range(4):

            @pl.when(rb == case)
            def _():
                for s in range(STEPS):
                    out[s, pl.ds(case * RB, RB), :] = total[pl.ds(b * USED + s * RB, RB), :]


def per_device(amplitudes, integrals, row_offsets, panel_owner):
    own, other = gather_panels(amplitudes, panel_owner)
    def codes(*n):
        return jax.ShapeDtypeStruct(n + (TALL, SLOT), jnp.int16)

    def cost(n):
        return pl.CostEstimate(
            flops=2 * TALL * 4 * KB * n * SLOT, bytes_accessed=8 * KB * n * SLOT, transcendentals=0
        )

    def room(n):
        return [pltpu.VMEM((n * SLOT, 4 * KB), jnp.bfloat16)]

    def wide(n):
        return [pltpu.VMEM((TALL, n * SLOT), jnp.float32)]

    def sems(n):
        return [pltpu.SemaphoreType.DMA((n,))]

    far, near = len(FAR), len(NEAR)
    away_far, left = pl.pallas_call(
        away_far_kernel,
        out_shape=[codes(far), jax.ShapeDtypeStruct((TALL, 4 * KB), jnp.bfloat16)],
        in_specs=[VMEM, VMEM, HBM],
        out_specs=[VMEM, VMEM],
        scratch_shapes=room(far) + wide(far) + sems(far),
        compiler_params=LARGE,
        cost_estimate=cost(far),
        name="away_far",
    )(own, other, integrals)
    got_far = lax.ppermute(away_far, "yl", shift(2, 1))
    away_near = pl.pallas_call(
        away_near_kernel,
        out_shape=codes(near),
        in_specs=[VMEM, HBM],
        out_specs=VMEM,
        scratch_shapes=room(near) + wide(near) + sems(near),
        compiler_params=LARGE,
        cost_estimate=cost(near),
        name="away_near",
    )(left, integrals)
    kept = pl.pallas_call(
        home_kernel,
        out_shape=jax.ShapeDtypeStruct((TALL, 8 * SLOT), jnp.float32),
        in_specs=[VMEM, HBM, ANY],
        out_specs=VMEM,
        scratch_shapes=room(8) + sems(8),
        compiler_params=LARGE,
        cost_estimate=cost(8),
        name="home",
    )(left, integrals, away_near)
    got_far, away_near, kept = lax.optimization_barrier((got_far, away_near, kept))
    got_near = lax.ppermute(away_near, "yl", shift(2, 1))
    met_far = pl.pallas_call(
        meet_far_kernel,
        out_shape=[codes()] * far,
        in_specs=[VMEM, VMEM],
        out_specs=[VMEM] * far,
        compiler_params=SMALL,
        name="meet_far",
    )(got_far, kept)
    met_near = pl.pallas_call(
        meet_near_kernel,
        out_shape=[codes()] * (near - 1) + [jax.ShapeDtypeStruct((TALL, SLOT), jnp.float32)],
        in_specs=[VMEM, VMEM, ANY],
        out_specs=[VMEM] * near,
        compiler_params=SMALL,
        name="meet_near",
    )(got_near, kept, met_far[0])
    got = [lax.ppermute(c, "z", shift(8, d)) for c, d in zip(met_far, FAR)]
    got += [lax.ppermute(c, "z", shift(8, d)) for c, d in zip(met_near, NEAR[:-1])]
    return pl.pallas_call(
        sum_kernel,
        out_shape=jax.ShapeDtypeStruct((STEPS, 4 * RB, SLOT), jnp.float32),
        in_specs=[SMEM] + [VMEM] * 8,
        out_specs=VMEM,
        scratch_shapes=[pltpu.VMEM((TALL, SLOT), jnp.float32)],
        compiler_params=SMALL,
        name="sum",
    )(row_offsets, *got, met_near[-1])


def solution(mesh):
    fine = Mesh(mesh.devices.reshape(2, 4, 2, 2, 8), ROW + COL)
    return jax.shard_map(
        per_device,
        mesh=fine,
        in_specs=(P(ROW, COL), P(ROW, COL), P(), P()),
        out_specs=P(None, None, ROW + COL),
        check_vma=False,
    )
```

```python
import jax
import jax.numpy as jnp
from jax import lax
from jax.experimental import pallas as pl
from jax.experimental.pallas import tpu as pltpu
from jax.sharding import Mesh, PartitionSpec as P

STEPS = 3
ROW = ("yh", "x", "core")
COL = ("yl", "z")
SLOT = 128
RB = 25
USED = STEPS * RB
BLK = 80
ROWS = 4 * USED
TALL = 304
GROUPS = ((0, 80), (80, 160), (160, 240), (240, TALL))
KB = 640
TILES = KB // 128
FAR = (4, 3, 5)
NEAR = (2, 6, 1, 7, 0)
CODE = 2.0**14 * (1 - 2.0**-13)
VMEM = pl.BlockSpec(memory_space=pltpu.VMEM)
SMEM = pl.BlockSpec(memory_space=pltpu.SMEM)
HBM = pl.BlockSpec(memory_space=pltpu.HBM)
ANY = pl.BlockSpec(memory_space=pl.ANY)
SMALL = pltpu.CompilerParams(vmem_limit_bytes=8 << 20)
LARGE = pltpu.CompilerParams(vmem_limit_bytes=46 << 20)


def shift(size, by):
    return [(i, (i + by) % size) for i in range(size)]


def cut_kernel(panel, pieces):
    for yh in range(2):
        for core in range(2):
            for x in range(4):
                for t in range(TILES):
                    block = panel[pl.ds((yh * 2 + core) * RB, RB), pl.ds(x * KB + t * 128, 128)]
                    pieces[yh * 8 + x * 2 + core, pl.ds(t * RB, RB), :] = block


def pick_kernel(owner, offsets, held, mine, live):
    yh, x, core, yl, z = (lax.axis_index(a) for a in ROW + COL)
    row = (yh * 4 + x) * 2 + core
    slot = (yl * 8 + z) * SLOT + lax.broadcasted_iota(jnp.int32, (1, SLOT), 1)
    live[...] = (slot < offsets[row + 1] - offsets[row]).astype(jnp.float32)
    for s in range(STEPS):
        for t in range(TILES):
            mine[pl.ds(s * RB, RB), pl.ds(t * 128, 128)] = held[owner[s], pl.ds(t * RB, RB), :]


def gather_panels(amplitudes, row_offsets, panel_owner):
    pieces = pl.pallas_call(
        cut_kernel,
        out_shape=jax.ShapeDtypeStruct((16, 128, 128), jnp.bfloat16),
        in_specs=[VMEM],
        out_specs=VMEM,
        compiler_params=SMALL,
        name="cut",
    )(amplitudes)
    held = lax.all_to_all(pieces, ROW, 0, 0)
    mine, live = pl.pallas_call(
        pick_kernel,
        out_shape=[jax.ShapeDtypeStruct((BLK, KB), jnp.bfloat16), jax.ShapeDtypeStruct((1, SLOT), jnp.float32)],
        in_specs=[SMEM, SMEM, VMEM],
        out_specs=[VMEM, VMEM],
        compiler_params=SMALL,
        name="pick",
    )(panel_owner, row_offsets, held)
    across = lax.ppermute(mine, "yh", shift(2, 1))
    straight = [mine] + [lax.ppermute(mine, "x", shift(4, d)) for d in range(1, 4)]
    turned = [across] + [lax.ppermute(across, "x", shift(4, d)) for d in range(1, 4)]
    turned[2] = lax.ppermute(straight[2], "yh", shift(2, 1))
    own = [jnp.stack(straight), jnp.stack(turned)]
    return live, own + [lax.ppermute(four, "core", shift(2, 1)) for four in own]


def last_rows():
    return lax.broadcasted_iota(jnp.int32, (16, SLOT), 0) + TALL - 16


def encode(rows, out, at):
    exponents = []
    for lo, hi in GROUPS:
        block = rows(lo, hi)
        largest = jnp.max(jnp.abs(block), axis=0, keepdims=True)
        exponent = jnp.floor(jnp.log2(jnp.maximum(largest, 2.0**-100)))
        exponents.append(exponent)
        code = jnp.round(block * (jnp.exp2(-exponent) * CODE))
        if hi == TALL:
            last = code[-16:]
            for g, e in enumerate(exponents):
                last = jnp.where(last_rows() == ROWS + g, e, last)
            code = jnp.concatenate([code[:-16], last])
        rows_out = (pl.ds(lo, hi - lo), slice(None))
        out[rows_out if at is None else (at,) + rows_out] = code.astype(jnp.int32).astype(jnp.int16)


def decode(codes, lo, hi, group):
    scale = jnp.exp2(codes[pl.ds(TALL - 16, 16), :].astype(jnp.int32).astype(jnp.float32)[12 + group : 13 + group])
    return codes[pl.ds(lo, hi - lo), :].astype(jnp.int32).astype(jnp.float32) * (scale * (1 / CODE))


def fetch(integrals, slabs, sems, yl, places):
    z = lax.axis_index("z")
    copies = []
    for n, d in enumerate(places):
        rows = pl.ds(pl.multiple_of((yl * 8 + lax.rem(z + d, 8)) * SLOT, SLOT), SLOT)
        copies.append(pltpu.make_async_copy(integrals.at[rows], slabs.at[pl.ds(n * SLOT, SLOT)], sems.at[n]))
        copies[-1].start()
    return copies


def multiply(left, slabs, copies, acc):
    count, n = len(copies), 0
    for some in (count - 3 * ((count - 1) // 3),) + (3,) * ((count - 1) // 3):
        for copy in copies[n : n + some]:
            copy.wait()
        columns = pl.ds(n * SLOT, some * SLOT)
        acc[:, columns] = lax.dot_general(
            left[...], slabs[columns, :], (((1,), (1,)), ((), ())), preferred_element_type=jnp.float32
        )
        n += some


def encode_all(acc, out):
    for n in range(out.shape[0]):
        encode(lambda lo, hi: acc[pl.ds(lo, hi - lo), pl.ds(n * SLOT, SLOT)], out, n)


def away_far_kernel(a, b, c, d, integrals, out, left, slabs, acc, sems):
    x = lax.axis_index("x")
    copies = fetch(integrals, slabs, sems, 1 - lax.axis_index("yl"), FAR)
    left[pl.ds(TALL - 16, 16), :] = jnp.zeros((16, 4 * KB), jnp.bfloat16)
    for back in range(4):
        columns = pl.ds(pl.multiple_of(lax.rem(x - back + 4, 4) * KB, KB), KB)
        for n, piece in enumerate((a, b, c, d)):
            left[pl.ds(n * USED, USED), columns] = piece[back, pl.ds(0, USED), :]
    multiply(left, slabs, copies, acc)
    encode_all(acc, out)


def away_near_kernel(left, integrals, out, slabs, acc, sems):
    multiply(left, slabs, fetch(integrals, slabs, sems, 1 - lax.axis_index("yl"), NEAR), acc)
    encode_all(acc, out)


def home_kernel(left, integrals, after, out, slabs, sems):
    multiply(left, slabs, fetch(integrals, slabs, sems, lax.axis_index("yl"), FAR + NEAR), out)


def added(got, kept, n, column):
    sums = []
    for g, (lo, hi) in enumerate(GROUPS):
        part = kept[pl.ds(lo, hi - lo), pl.ds(column * SLOT, SLOT)] + decode(got.at[n], lo, hi, g)
        if hi == TALL:
            part = jnp.concatenate([part[:-16], jnp.where(last_rows() < ROWS, part[-16:], 0.0)])
        sums.append(part)
    return sums


def meet_far_kernel(got, kept, *outs):
    for n, out in enumerate(outs):
        sums = added(got, kept, n, n)
        encode(lambda lo, hi: sums[GROUPS.index((lo, hi))], out, None)


def meet_near_kernel(got, kept, after, *outs):
    for n, out in enumerate(outs):
        sums = added(got, kept, n, len(FAR) + n)
        if NEAR[n] == 0:
            for (lo, hi), part in zip(GROUPS, sums):
                out[pl.ds(lo, hi - lo), :] = part
        else:
            encode(lambda lo, hi: sums[GROUPS.index((lo, hi))], out, None)


def sum_kernel(*refs):
    *got, kept, live, out, total = refs
    yh, core = lax.axis_index("yh"), lax.axis_index("core")
    for g, (lo, hi) in enumerate(GROUPS):
        part = kept[pl.ds(lo, hi - lo), :]
        for codes in got:
            part = part + decode(codes, lo, hi, g)
        total[pl.ds(lo, hi - lo), :] = part * live[...]
    for b in range(4):
        rb = lax.rem(yh + b % 2, 2) * 2 + lax.rem(core + b // 2, 2)
        for case in range(4):

            @pl.when(rb == case)
            def _():
                for s in range(STEPS):
                    out[s, pl.ds(case * RB, RB), :] = total[pl.ds(b * USED + s * RB, RB), :]


def per_device(amplitudes, integrals, row_offsets, panel_owner):
    live, panels = gather_panels(amplitudes, row_offsets, panel_owner)
    def codes(*n):
        return jax.ShapeDtypeStruct(n + (TALL, SLOT), jnp.int16)

    def cost(n):
        return pl.CostEstimate(
            flops=2 * TALL * 4 * KB * n * SLOT, bytes_accessed=8 * KB * n * SLOT, transcendentals=0
        )

    def room(n):
        return [pltpu.VMEM((n * SLOT, 4 * KB), jnp.bfloat16)]

    def wide(n):
        return [pltpu.VMEM((TALL, n * SLOT), jnp.float32)]

    def sems(n):
        return [pltpu.SemaphoreType.DMA((n,))]

    far, near = len(FAR), len(NEAR)
    away_far, left = pl.pallas_call(
        away_far_kernel,
        out_shape=[codes(far), jax.ShapeDtypeStruct((TALL, 4 * KB), jnp.bfloat16)],
        in_specs=[VMEM, VMEM, VMEM, VMEM, HBM],
        out_specs=[VMEM, VMEM],
        scratch_shapes=room(far) + wide(far) + sems(far),
        compiler_params=LARGE,
        cost_estimate=cost(far),
        name="away_far",
    )(*panels, integrals)
    got_far = lax.ppermute(away_far, "yl", shift(2, 1))
    away_near = pl.pallas_call(
        away_near_kernel,
        out_shape=codes(near),
        in_specs=[VMEM, HBM],
        out_specs=VMEM,
        scratch_shapes=room(near) + wide(near) + sems(near),
        compiler_params=LARGE,
        cost_estimate=cost(near),
        name="away_near",
    )(left, integrals)
    kept = pl.pallas_call(
        home_kernel,
        out_shape=jax.ShapeDtypeStruct((TALL, 8 * SLOT), jnp.float32),
        in_specs=[VMEM, HBM, ANY],
        out_specs=VMEM,
        scratch_shapes=room(8) + sems(8),
        compiler_params=LARGE,
        cost_estimate=cost(8),
        name="home",
    )(left, integrals, away_near)
    got_far, away_near, kept = lax.optimization_barrier((got_far, away_near, kept))
    got_near = lax.ppermute(away_near, "yl", shift(2, 1))
    met_far = pl.pallas_call(
        meet_far_kernel,
        out_shape=[codes()] * far,
        in_specs=[VMEM, VMEM],
        out_specs=[VMEM] * far,
        compiler_params=SMALL,
        name="meet_far",
    )(got_far, kept)
    met_near = pl.pallas_call(
        meet_near_kernel,
        out_shape=[codes()] * (near - 1) + [jax.ShapeDtypeStruct((TALL, SLOT), jnp.float32)],
        in_specs=[VMEM, VMEM, ANY],
        out_specs=[VMEM] * near,
        compiler_params=SMALL,
        name="meet_near",
    )(got_near, kept, met_far[0])
    got = [lax.ppermute(c, "z", shift(8, d)) for c, d in zip(met_far, FAR)]
    got += [lax.ppermute(c, "z", shift(8, d)) for c, d in zip(met_near, NEAR[:-1])]
    return pl.pallas_call(
        sum_kernel,
        out_shape=jax.ShapeDtypeStruct((STEPS, 4 * RB, SLOT), jnp.float32),
        in_specs=[VMEM] * 9,
        out_specs=VMEM,
        scratch_shapes=[pltpu.VMEM((TALL, SLOT), jnp.float32)],
        compiler_params=SMALL,
        name="sum",
    )(*got, met_near[-1], live)


def solution(mesh):
    fine = Mesh(mesh.devices.reshape(2, 4, 2, 2, 8), ROW + COL)
    return jax.shard_map(
        per_device,
        mesh=fine,
        in_specs=(P(ROW, COL), P(ROW, COL), P(), P()),
        out_specs=P(None, None, ROW + COL),
        check_vma=False,
    )
```

```python
import jax
import jax.numpy as jnp
from jax import lax
from jax.experimental import pallas as pl
from jax.experimental.pallas import tpu as pltpu
from jax.sharding import Mesh, PartitionSpec as P

STEPS = 3
ROW = ("yh", "x", "core")
COL = ("yl", "z")
SLOT = 128
RB = 25
USED = STEPS * RB
BLK = 80
ROWS = 4 * USED
TALL = 304
GROUPS = ((0, 80), (80, 160), (160, 240), (240, TALL))
KB = 640
TILES = KB // 128
FAR = (4, 3, 5)
NEAR = (2, 6, 1, 7, 0)
CODE = 2.0**14 * (1 - 2.0**-13)
VMEM = pl.BlockSpec(memory_space=pltpu.VMEM)
SMEM = pl.BlockSpec(memory_space=pltpu.SMEM)
HBM = pl.BlockSpec(memory_space=pltpu.HBM)
ANY = pl.BlockSpec(memory_space=pl.ANY)
SMALL = pltpu.CompilerParams(vmem_limit_bytes=8 << 20)
LARGE = pltpu.CompilerParams(vmem_limit_bytes=46 << 20)


def shift(size, by):
    return [(i, (i + by) % size) for i in range(size)]


def cut_kernel(panel, pieces, near, sems):
    copies = []
    for x in range(4):
        columns = pl.ds(x * KB, KB)
        copies.append(pltpu.make_async_copy(panel.at[:, columns], near.at[:, columns], sems.at[x]))
        copies[-1].start()
    for x in range(4):
        copies[x].wait()
        for yh in range(2):
            for core in range(2):
                for t in range(TILES):
                    block = near[pl.ds((yh * 2 + core) * RB, RB), pl.ds(x * KB + t * 128, 128)]
                    pieces[yh * 8 + x * 2 + core, pl.ds(t * RB, RB), :] = block


def pick_kernel(owner, offsets, held, mine, live):
    yh, x, core, yl, z = (lax.axis_index(a) for a in ROW + COL)
    row = (yh * 4 + x) * 2 + core
    slot = (yl * 8 + z) * SLOT + lax.broadcasted_iota(jnp.int32, (1, SLOT), 1)
    live[...] = (slot < offsets[row + 1] - offsets[row]).astype(jnp.float32)
    for s in range(STEPS):
        for t in range(TILES):
            mine[pl.ds(s * RB, RB), pl.ds(t * 128, 128)] = held[owner[s], pl.ds(t * RB, RB), :]


def gather_panels(amplitudes, row_offsets, panel_owner):
    pieces = pl.pallas_call(
        cut_kernel,
        out_shape=jax.ShapeDtypeStruct((16, 128, 128), jnp.bfloat16),
        in_specs=[HBM],
        out_specs=VMEM,
        scratch_shapes=[pltpu.VMEM((4 * RB, 4 * KB), jnp.bfloat16), pltpu.SemaphoreType.DMA((4,))],
        compiler_params=pltpu.CompilerParams(vmem_limit_bytes=61 << 20),
        name="cut",
    )(amplitudes)
    held = lax.all_to_all(pieces, ROW, 0, 0)
    mine, live = pl.pallas_call(
        pick_kernel,
        out_shape=[jax.ShapeDtypeStruct((BLK, KB), jnp.bfloat16), jax.ShapeDtypeStruct((1, SLOT), jnp.float32)],
        in_specs=[SMEM, SMEM, VMEM],
        out_specs=[VMEM, VMEM],
        compiler_params=SMALL,
        name="pick",
    )(panel_owner, row_offsets, held)
    across = lax.ppermute(mine, "yh", shift(2, 1))
    straight = [mine] + [lax.ppermute(mine, "x", shift(4, d)) for d in range(1, 4)]
    turned = [across] + [lax.ppermute(across, "x", shift(4, d)) for d in range(1, 4)]
    turned[2] = lax.ppermute(straight[2], "yh", shift(2, 1))
    own = [jnp.stack(straight), jnp.stack(turned)]
    return live, own + [lax.ppermute(four, "core", shift(2, 1)) for four in own]


def last_rows():
    return lax.broadcasted_iota(jnp.int32, (16, SLOT), 0) + TALL - 16


def encode(rows, out, at):
    exponents = []
    for lo, hi in GROUPS:
        block = rows(lo, hi)
        largest = jnp.max(jnp.abs(block), axis=0, keepdims=True)
        exponent = jnp.floor(jnp.log2(jnp.maximum(largest, 2.0**-100)))
        exponents.append(exponent)
        code = jnp.round(block * (jnp.exp2(-exponent) * CODE))
        if hi == TALL:
            last = code[-16:]
            for g, e in enumerate(exponents):
                last = jnp.where(last_rows() == ROWS + g, e, last)
            code = jnp.concatenate([code[:-16], last])
        rows_out = (pl.ds(lo, hi - lo), slice(None))
        out[rows_out if at is None else (at,) + rows_out] = code.astype(jnp.int32).astype(jnp.int16)


def decode(codes, lo, hi, group):
    scale = jnp.exp2(codes[pl.ds(TALL - 16, 16), :].astype(jnp.int32).astype(jnp.float32)[12 + group : 13 + group])
    return codes[pl.ds(lo, hi - lo), :].astype(jnp.int32).astype(jnp.float32) * (scale * (1 / CODE))


def fetch(integrals, slabs, sems, yl, places):
    z = lax.axis_index("z")
    copies = []
    for n, d in enumerate(places):
        rows = pl.ds(pl.multiple_of((yl * 8 + lax.rem(z + d, 8)) * SLOT, SLOT), SLOT)
        copies.append(pltpu.make_async_copy(integrals.at[rows], slabs.at[pl.ds(n * SLOT, SLOT)], sems.at[n]))
        copies[-1].start()
    return copies


def multiply(left, slabs, copies, acc):
    count, n = len(copies), 0
    for some in (count - 3 * ((count - 1) // 3),) + (3,) * ((count - 1) // 3):
        for copy in copies[n : n + some]:
            copy.wait()
        columns = pl.ds(n * SLOT, some * SLOT)
        acc[:, columns] = lax.dot_general(
            left[...], slabs[columns, :], (((1,), (1,)), ((), ())), preferred_element_type=jnp.float32
        )
        n += some


def encode_all(acc, out):
    for n in range(out.shape[0]):
        encode(lambda lo, hi: acc[pl.ds(lo, hi - lo), pl.ds(n * SLOT, SLOT)], out, n)


def away_far_kernel(a, b, c, d, integrals, out, left, slabs, acc, sems):
    x = lax.axis_index("x")
    copies = fetch(integrals, slabs, sems, 1 - lax.axis_index("yl"), FAR)
    left[pl.ds(TALL - 16, 16), :] = jnp.zeros((16, 4 * KB), jnp.bfloat16)
    for back in range(4):
        columns = pl.ds(pl.multiple_of(lax.rem(x - back + 4, 4) * KB, KB), KB)
        for n, piece in enumerate((a, b, c, d)):
            left[pl.ds(n * USED, USED), columns] = piece[back, pl.ds(0, USED), :]
    multiply(left, slabs, copies, acc)
    encode_all(acc, out)


def away_near_kernel(left, integrals, out, slabs, acc, sems):
    multiply(left, slabs, fetch(integrals, slabs, sems, 1 - lax.axis_index("yl"), NEAR), acc)
    encode_all(acc, out)


def home_kernel(left, integrals, after, out, slabs, sems):
    multiply(left, slabs, fetch(integrals, slabs, sems, lax.axis_index("yl"), FAR + NEAR), out)


def added(got, kept, n, column):
    sums = []
    for g, (lo, hi) in enumerate(GROUPS):
        part = kept[pl.ds(lo, hi - lo), pl.ds(column * SLOT, SLOT)] + decode(got.at[n], lo, hi, g)
        if hi == TALL:
            part = jnp.concatenate([part[:-16], jnp.where(last_rows() < ROWS, part[-16:], 0.0)])
        sums.append(part)
    return sums


def meet_far_kernel(got, kept, *outs):
    for n, out in enumerate(outs):
        sums = added(got, kept, n, n)
        encode(lambda lo, hi: sums[GROUPS.index((lo, hi))], out, None)


def meet_near_kernel(got, kept, after, *outs):
    for n, out in enumerate(outs):
        sums = added(got, kept, n, len(FAR) + n)
        if NEAR[n] == 0:
            for (lo, hi), part in zip(GROUPS, sums):
                out[pl.ds(lo, hi - lo), :] = part
        else:
            encode(lambda lo, hi: sums[GROUPS.index((lo, hi))], out, None)


def sum_kernel(*refs):
    *got, kept, live, out, total = refs
    yh, core = lax.axis_index("yh"), lax.axis_index("core")
    for g, (lo, hi) in enumerate(GROUPS):
        part = kept[pl.ds(lo, hi - lo), :]
        for codes in got:
            part = part + decode(codes, lo, hi, g)
        total[pl.ds(lo, hi - lo), :] = part * live[...]
    for b in range(4):
        rb = lax.rem(yh + b % 2, 2) * 2 + lax.rem(core + b // 2, 2)
        for case in range(4):

            @pl.when(rb == case)
            def _():
                for s in range(STEPS):
                    out[s, pl.ds(case * RB, RB), :] = total[pl.ds(b * USED + s * RB, RB), :]


def per_device(amplitudes, integrals, row_offsets, panel_owner):
    live, panels = gather_panels(amplitudes, row_offsets, panel_owner)
    def codes(*n):
        return jax.ShapeDtypeStruct(n + (TALL, SLOT), jnp.int16)

    def cost(n):
        return pl.CostEstimate(
            flops=2 * TALL * 4 * KB * n * SLOT, bytes_accessed=8 * KB * n * SLOT, transcendentals=0
        )

    def room(n):
        return [pltpu.VMEM((n * SLOT, 4 * KB), jnp.bfloat16)]

    def wide(n):
        return [pltpu.VMEM((TALL, n * SLOT), jnp.float32)]

    def sems(n):
        return [pltpu.SemaphoreType.DMA((n,))]

    far, near = len(FAR), len(NEAR)
    away_far, left = pl.pallas_call(
        away_far_kernel,
        out_shape=[codes(far), jax.ShapeDtypeStruct((TALL, 4 * KB), jnp.bfloat16)],
        in_specs=[VMEM, VMEM, VMEM, VMEM, HBM],
        out_specs=[VMEM, VMEM],
        scratch_shapes=room(far) + wide(far) + sems(far),
        compiler_params=LARGE,
        cost_estimate=cost(far),
        name="away_far",
    )(*panels, integrals)
    got_far = lax.ppermute(away_far, "yl", shift(2, 1))
    away_near = pl.pallas_call(
        away_near_kernel,
        out_shape=codes(near),
        in_specs=[VMEM, HBM],
        out_specs=VMEM,
        scratch_shapes=room(near) + wide(near) + sems(near),
        compiler_params=LARGE,
        cost_estimate=cost(near),
        name="away_near",
    )(left, integrals)
    kept = pl.pallas_call(
        home_kernel,
        out_shape=jax.ShapeDtypeStruct((TALL, 8 * SLOT), jnp.float32),
        in_specs=[VMEM, HBM, ANY],
        out_specs=VMEM,
        scratch_shapes=room(8) + sems(8),
        compiler_params=LARGE,
        cost_estimate=cost(8),
        name="home",
    )(left, integrals, away_near)
    got_far, away_near, kept = lax.optimization_barrier((got_far, away_near, kept))
    got_near = lax.ppermute(away_near, "yl", shift(2, 1))
    met_far = pl.pallas_call(
        meet_far_kernel,
        out_shape=[codes()] * far,
        in_specs=[VMEM, VMEM],
        out_specs=[VMEM] * far,
        compiler_params=SMALL,
        name="meet_far",
    )(got_far, kept)
    met_near = pl.pallas_call(
        meet_near_kernel,
        out_shape=[codes()] * (near - 1) + [jax.ShapeDtypeStruct((TALL, SLOT), jnp.float32)],
        in_specs=[VMEM, VMEM, ANY],
        out_specs=[VMEM] * near,
        compiler_params=SMALL,
        name="meet_near",
    )(got_near, kept, met_far[0])
    got = [lax.ppermute(c, "z", shift(8, d)) for c, d in zip(met_far, FAR)]
    got += [lax.ppermute(c, "z", shift(8, d)) for c, d in zip(met_near, NEAR[:-1])]
    return pl.pallas_call(
        sum_kernel,
        out_shape=jax.ShapeDtypeStruct((STEPS, 4 * RB, SLOT), jnp.float32),
        in_specs=[VMEM] * 9,
        out_specs=VMEM,
        scratch_shapes=[pltpu.VMEM((TALL, SLOT), jnp.float32)],
        compiler_params=SMALL,
        name="sum",
    )(*got, met_near[-1], live)


def solution(mesh):
    fine = Mesh(mesh.devices.reshape(2, 4, 2, 2, 8), ROW + COL)
    return jax.shard_map(
        per_device,
        mesh=fine,
        in_specs=(P(ROW, COL), P(ROW, COL), P(), P()),
        out_specs=P(None, None, ROW + COL),
        check_vma=False,
    )
```
